256 devices in a mesh: row: 16 (over z, x_lo), col: 16 (over y, x_hi, core).
Axes of the slice: x: 4 (x_hi: 2, x_lo: 2; x = x_hi * 2 + x_lo), y: 4, z: 8, core: 2. Of those that a mesh axis runs over, the one named last changes fastest.
Arguments:
- velocity: bfloat16 [384, 640, 640], P('row', 'col'), may hold values from -6 to 6
- trans_x: bfloat16 [384, 640, 640], P('row', 'col'), may hold values from -6 to 6
- trans_y: bfloat16 [384, 640, 640], P('row', 'col'), may hold values from -6 to 6
- trans_z: bfloat16 [384, 640, 640], P('row', 'col'), may hold values from -6 to 6
- deriv_x1: bfloat16 [640, 640], replicated, may hold values from -0.25 to 0.25
- deriv_x2: bfloat16 [640, 640], replicated, may hold values from -0.25 to 0.25
- deriv_y1: bfloat16 [384, 384], replicated, may hold values from -0.3125 to 0.3125
- deriv_y2: bfloat16 [384, 384], replicated, may hold values from -0.3125 to 0.3125
- deriv_z1: bfloat16 [640, 640], replicated, may hold values from -0.25 to 0.25
- deriv_z2: bfloat16 [640, 640], replicated, may hold values from -0.25 to 0.25
- metric_one: float32 [384], replicated, may hold values from 0.5 to 2
- metric_two: float32 [384], replicated, may hold values from -1 to 1
Outputs:
- rhs: float32 [384, 640, 640], P('row', 'col')
- advanced: bfloat16 [384, 640, 640], P('row', 'col')
The draws below stay inside these ranges and needn't reach their ends.
All inputs are finite; a program needn't handle non-finite values.
Results may differ from the reference program's by a relative error of at most 0.0038.
Values may be sent and summed in bfloat16 or wider, within the bound.
A program may use at most 128 MiB of HBM per device.

```python
import math
import jax
import jax.numpy as jnp

NX = 640
NY = 384
NZ = 640


def levels(stream_key, extent, split, smallest, largest):
    loudness, own = 1.0, jax.random.fold_in(stream_key, 6)
    for dim, blocks in split:
        steps = jnp.exp(jax.random.uniform(jax.random.fold_in(own, dim), (blocks,), jnp.float32, smallest / len(split), largest / len(split)))
        loudness = loudness * jnp.repeat(steps, extent[dim] // blocks).reshape([-1 if axis == dim else 1 for axis in range(len(extent))])
    return loudness


def centred(own_key, dims, deviation, bound, pieces=(), dtype=jnp.bfloat16):
    entries = jax.random.normal(own_key, dims, jnp.float32) * deviation
    if len(pieces) > 0:
        entries = levels(own_key, dims, pieces, -0.22, 0.18) * entries
    return jnp.clip(entries, min=-bound, max=bound).astype(dtype)


def setup_inputs(seed: int = 0) -> dict:
    arg_keys = jax.random.split(jax.random.key(seed), 13)
    velocity = centred(arg_keys[0], (NY, NZ, NX), 1.0, 6.0, ((0, 16), (1, 16)))
    trans_x = centred(arg_keys[1], (NY, NZ, NX), 1.0, 6.0, ((0, 16), (1, 16)))
    trans_y = centred(arg_keys[2], (NY, NZ, NX), 1.0, 6.0, ((0, 16), (1, 16)))
    trans_z = centred(arg_keys[3], (NY, NZ, NX), 1.0, 6.0, ((0, 16), (1, 16)))
    deriv_x1 = centred(arg_keys[4], (NX, NX), NX ** -0.5, 0.25)
    deriv_x2 = centred(arg_keys[5], (NX, NX), NX ** -0.5, 0.25)
    deriv_y1 = centred(arg_keys[6], (NY, NY), NY ** -0.5, 0.3125)
    deriv_y2 = centred(arg_keys[7], (NY, NY), NY ** -0.5, 0.3125)
    deriv_z1 = centred(arg_keys[8], (NZ, NZ), NZ ** -0.5, 0.25)
    deriv_z2 = centred(arg_keys[9], (NZ, NZ), NZ ** -0.5, 0.25)
    metric_one = jnp.clip(jnp.exp(jax.random.uniform(arg_keys[10], (NY,), jnp.float32, math.log(0.5), math.log(2.0))), 0.5, 2.0)
    metric_two = jnp.clip(jax.random.uniform(arg_keys[11], (NY,), jnp.float32, -1.0, 1.0), -1.0, 1.0)
    return {"velocity": velocity, "trans_x": trans_x, "trans_y": trans_y, "trans_z": trans_z, "deriv_x1": deriv_x1, "deriv_x2": deriv_x2, "deriv_y1": deriv_y1, "deriv_y2": deriv_y2, "deriv_z1": deriv_z1, "deriv_z2": deriv_z2, "metric_one": metric_one, "metric_two": metric_two}


def along_x(matrix, field):
    return jnp.einsum('wx,yzx->yzw', matrix.astype(jnp.float32), field)


def along_y(matrix, field):
    return jnp.einsum('vy,yzx->vzx', matrix.astype(jnp.float32), field)


def along_z(matrix, field):
    return jnp.einsum('wz,yzx->ywx', matrix.astype(jnp.float32), field)


def reference(velocity, trans_x, trans_y, trans_z, deriv_x1, deriv_x2, deriv_y1, deriv_y2, deriv_z1, deriv_z2, metric_one, metric_two):
    field = velocity.astype(jnp.float32)
    rhs = -trans_x.astype(jnp.float32) * along_x(deriv_x1, field) + 0.5 * along_x(deriv_x2, field)
    first_y = along_y(deriv_y1, field)
    second_y = along_y(deriv_y2, field)
    scale_one = metric_one[:, None, None]
    scale_two = metric_two[:, None, None]
    rhs = rhs + (-trans_y.astype(jnp.float32) * scale_one * first_y + 0.5 * (scale_one * scale_one * second_y + scale_two * first_y))
    rhs = rhs + (-trans_z.astype(jnp.float32) * along_z(deriv_z1, field) + 0.5 * along_z(deriv_z2, field))
    advanced = (field + 0.3 * rhs).astype(jnp.bfloat16)
    return rhs, advanced
```

```python
import jax
import jax.numpy as jnp
from jax import lax
from jax.sharding import PartitionSpec as P


def body(
    velocity,
    trans_x,
    trans_y,
    trans_z,
    deriv_x1,
    deriv_x2,
    deriv_y1,
    deriv_y2,
    deriv_z1,
    deriv_z2,
    metric_one,
    metric_two,
):
    ylocal, zlocal, xwidth = velocity.shape
    rows_count = lax.axis_size("row")
    cols_count = lax.axis_size("col")

    block_cols = zlocal * xwidth // rows_count
    both_y = jnp.stack([velocity, trans_y]).reshape(2, ylocal, rows_count, block_cols)
    lines_y = lax.all_to_all(both_y, "row", split_axis=2, concat_axis=1, tiled=True)
    total_y = lines_y.shape[1]
    lines_y = lines_y.reshape(2, total_y, block_cols)
    first_y = jnp.dot(deriv_y1, lines_y[0], preferred_element_type=jnp.float32)
    second_y = jnp.dot(deriv_y2, lines_y[0], preferred_element_type=jnp.float32)
    scale_one = metric_one[:, None]
    scale_two = metric_two[:, None]
    term_y = -lines_y[1].astype(jnp.float32) * scale_one * first_y + 0.5 * (
        scale_one * scale_one * second_y + scale_two * first_y
    )
    home_y = lax.all_to_all(
        term_y.astype(jnp.bfloat16).reshape(total_y, 1, block_cols),
        "row",
        split_axis=0,
        concat_axis=1,
        tiled=True,
    )
    home_y = home_y.reshape(ylocal, zlocal, xwidth)

    per_dev = -(-ylocal // cols_count)
    ypad = per_dev * cols_count
    both_z = jnp.stack([velocity, trans_z])
    both_z = jnp.pad(both_z, ((0, 0), (0, ypad - ylocal), (0, 0), (0, 0)))
    lines_z = lax.all_to_all(both_z, "col", split_axis=1, concat_axis=2, tiled=True)
    first_z = jnp.einsum("wz,yzx->ywx", deriv_z1, lines_z[0], preferred_element_type=jnp.float32)
    second_z = jnp.einsum("wz,yzx->ywx", deriv_z2, lines_z[0], preferred_element_type=jnp.float32)
    term_z = -lines_z[1].astype(jnp.float32) * first_z + 0.5 * second_z
    home_z = lax.all_to_all(
        term_z.astype(jnp.bfloat16), "col", split_axis=1, concat_axis=0, tiled=True
    )[:ylocal]

    first_x = jnp.einsum("wx,yzx->yzw", deriv_x1, velocity, preferred_element_type=jnp.float32)
    second_x = jnp.einsum("wx,yzx->yzw", deriv_x2, velocity, preferred_element_type=jnp.float32)
    term_x = -trans_x.astype(jnp.float32) * first_x + 0.5 * second_x

    rhs = term_x + home_y.astype(jnp.float32) + home_z.astype(jnp.float32)
    advanced = (velocity.astype(jnp.float32) + 0.3 * rhs).astype(jnp.bfloat16)
    return (rhs, advanced)


def solution(mesh):
    in_specs = (
        P("row", "col", None),
        P("row", "col", None),
        P("row", "col", None),
        P("row", "col", None),
        P(),
        P(),
        P(),
        P(),
        P(),
        P(),
        P(),
        P(),
    )
    out_specs = (P("row", "col", None), P("row", "col", None))
    return jax.shard_map(body, mesh=mesh, in_specs=in_specs, out_specs=out_specs, check_vma=False)
```
